512 devices in a mesh: seq: 64 (over y, z), chan: 8 (over x, core).
Axes of the slice: x: 4, y: 8, z: 8, core: 2. Of those that a mesh axis runs over, the one named last changes fastest.
Arguments:
- signal_in: bfloat16 [16384, 2048], P('seq', 'chan'), may hold values from -6 to 6
- value_in: bfloat16 [16384, 2048], P('seq', 'chan'), may hold values from -6 to 6
- gate_in: bfloat16 [16384, 2048], P('seq', 'chan'), may hold values from -6 to 6
- filter_taps: bfloat16 [16384, 2048], P('seq', 'chan'), may hold values from -0.046875 to 0.046875
- skip_gain: float32 [2048], P('chan'), may hold values from -1 to 1
- turn_starts: int32 [32], replicated, may hold values from 0 to 15999, as said below
- out_weight: bfloat16 [2048, 2048], P(None, 'chan'), may hold values from -0.125 to 0.125
Outputs:
- projected: bfloat16 [16384, 2048], P('seq', 'chan')
The draws below stay inside these ranges and needn't reach their ends.
Inputs may be any that keep to these rules, and one draw needn't show every extreme that they name: `turn_starts`: strictly rising; the first is 0; for k from 1 the k-th lies in [k * 512 - 512 // 4, k * 512 + 512 // 4); the last is (31) * 512 + 512 // 4 - 1.
All inputs are finite; a program needn't handle non-finite values.
Results may differ from the reference program's by a relative error of at most 0.0057.
Values may be sent and summed in bfloat16 or wider, within the bound.
A program may use at most 64 MiB of HBM per device.

```python
import jax
import jax.numpy as jnp
from jax import lax

D = 2048
TURN_SPAN = 512
SEQ = 16384
TURNS = 32


def draw_turn_starts(key, part):
    offsets = jax.random.randint(key, (TURNS,), 0, TURN_SPAN // 2, dtype=jnp.int32)
    slot_ids = jnp.arange(TURNS, dtype=jnp.int32)
    offsets = jnp.where(slot_ids == TURNS - 1, TURN_SPAN // 2 - 1, offsets)
    starts = slot_ids * TURN_SPAN - TURN_SPAN // 4 + offsets
    return jnp.where(slot_ids == 0, 0, starts).astype(jnp.int32)


def level_of(key, dims, shards, least, top_value):
    gain = 1.0
    for dim, parts in shards:
        heights = jax.random.uniform(jax.random.fold_in(jax.random.fold_in(key, 6), dim), (parts,), jnp.float32, least / len(shards), top_value / len(shards))
        gain = gain * jnp.repeat(jnp.exp(heights), dims[dim] // parts).reshape((-1,) + (1,) * (len(dims) - 1 - dim))
    return gain


def scatter_about(stream_key, shape, deviation, most, shards=(), held_as=jnp.bfloat16):
    array = deviation * jax.random.normal(stream_key, shape, jnp.float32)
    if shards:
        array = array * level_of(stream_key, shape, shards, -0.22, 0.18)
    return jnp.clip(array, -most, most).astype(held_as)


def setup_inputs(seed: int = 0) -> dict:
    splits = jax.random.split(jax.random.key(seed), 8)
    signal_in = scatter_about(splits[0], (SEQ, D), 1.0, 6.0, ((0, 64), (1, 8)))
    value_in = scatter_about(splits[1], (SEQ, D), 1.0, 6.0, ((0, 64), (1, 8)))
    gate_in = scatter_about(splits[2], (SEQ, D), 1.0, 6.0, ((0, 64), (1, 8)))
    filter_taps = scatter_about(splits[3], (SEQ, D), SEQ ** -0.5, 0.046875, ((0, 64), (1, 8)))
    skip_gain = jnp.clip(jax.random.uniform(splits[4], (D,), jnp.float32, -1.0, 1.0) * level_of(splits[4], (D,), ((0, 8),), -0.4, 0.0), -1.0, 1.0)
    turn_starts = draw_turn_starts(jax.random.fold_in(splits[7], 71), 0)
    out_weight = scatter_about(splits[6], (D, D), D ** -0.5, 0.125, ((1, 8),))
    return {"signal_in": signal_in, "value_in": value_in, "gate_in": gate_in, "filter_taps": filter_taps, "skip_gain": skip_gain, "turn_starts": turn_starts, "out_weight": out_weight}


def reference(signal_in, value_in, gate_in, filter_taps, skip_gain, turn_starts, out_weight):
    mixed_in = (signal_in.astype(jnp.float32) * value_in.astype(jnp.float32)).astype(jnp.bfloat16)
    total = mixed_in.shape[0]
    width = mixed_in.shape[1]
    block = min(256, width)
    stacked_signal = mixed_in.astype(jnp.float32).reshape(total, width // block, block).transpose(1, 0, 2)
    stacked_taps = filter_taps.astype(jnp.float32).reshape(total, width // block, block).transpose(1, 0, 2)

    def convolve(pair):
        signal_part, taps_part = pair
        spectrum = jnp.fft.rfft(signal_part, n=2 * total, axis=0) * jnp.fft.rfft(taps_part, n=2 * total, axis=0)
        return jnp.fft.irfft(spectrum, n=2 * total, axis=0)[:total]

    conv = lax.map(convolve, (stacked_signal, stacked_taps)).transpose(1, 0, 2).reshape(total, width)
    positions = jnp.arange(total, dtype=jnp.int32)
    counted = jnp.sum((turn_starts[None, :] <= positions[:, None]).astype(jnp.int32), axis=1)
    keep = jnp.where((counted - 1) % 2 == 0, 1.0, 0.0).astype(jnp.float32)
    gated = (gate_in.astype(jnp.float32) * keep[:, None] * (conv + skip_gain[None, :] * mixed_in.astype(jnp.float32))).astype(jnp.bfloat16)
    return jnp.dot(gated, out_weight.T, preferred_element_type=jnp.float32).astype(jnp.bfloat16)
```

```python
import functools
import math

import jax
import jax.numpy as jnp
import ml_dtypes
import numpy as np
from jax import lax
from jax.experimental import pallas as pl
from jax.experimental.pallas import tpu as pltpu
from jax.sharding import PartitionSpec as P

MESH = pl.DeviceIdType.MESH
F32 = jnp.float32
BF16 = jnp.bfloat16


def split_table(table):
    high = table.astype(ml_dtypes.bfloat16)
    low = (table - high.astype(np.float64)).astype(ml_dtypes.bfloat16)
    return high, low


def make_tables(groups, rows):
    length = 2 * groups * rows
    outer = np.arange(groups)
    inner = np.arange(rows)
    odd = 2 * outer + 1
    angle = 2.0 * math.pi * (odd[:, None] * outer[None, :] % (4 * groups)) / (4 * groups)
    first = np.concatenate([np.cos(angle), -np.sin(angle)], axis=0)
    twist = 2.0 * math.pi * (odd[:, None] * inner[None, :] % (2 * length)) / (2 * length)
    angle = 2.0 * math.pi * (inner[:, None] * inner[None, :] % rows) / rows
    cos, sin = np.cos(angle), np.sin(angle)
    middle = np.block([[cos, -sin], [sin, cos]])
    last = first.T * (2.0 / length)
    return (
        *split_table(first),
        *split_table(last),
        *split_table(middle),
        np.cos(twist).astype(np.float32),
        np.sin(twist).astype(np.float32),
    )


def halves(value):
    high = value.astype(BF16)
    return high, (value - high.astype(F32)).astype(BF16)


def dot(left, right, dims=((1,), (0,))):
    return lax.dot_general(left, right, (dims, ((), ())), preferred_element_type=F32)


def kernel(
    groups,
    chans,
    signal_ref,
    value_ref,
    gate_ref,
    taps_ref,
    skip_ref,
    starts_ref,
    weight_ref,
    first_hi_ref,
    first_lo_ref,
    last_hi_ref,
    last_lo_ref,
    mid_hi_ref,
    mid_lo_ref,
    twist_cos_ref,
    twist_sin_ref,
    out_ref,
    out_bf,
    in_bf,
    in_f32,
    spec_hi,
    spec_lo,
    back_f32,
    back_bf,
    home_bf,
    gated_all,
    weight_all,
    send_sem,
    recv_sem,
    back_send_sem,
    back_recv_sem,
    weight_send_sem,
    weight_recv_sem,
    gated_send_sem,
    gated_recv_sem,
):
    rows, width = signal_ref.shape
    own = width // groups
    half = rows // 2
    me = lax.axis_index("seq")
    mine = lax.axis_index("chan")
    core = lax.rem(mine, 2)
    sibling = mine + 1 - 2 * core

    barrier = pltpu.get_barrier_semaphore()

    @pl.loop(1, chans)
    def _(step):
        pl.semaphore_signal(
            barrier, inc=1, device_id={"chan": lax.rem(mine + step, chans)}, device_id_type=MESH
        )

    @pl.loop(1, groups)
    def _(step):
        pl.semaphore_signal(
            barrier, inc=1, device_id={"seq": lax.rem(me + step, groups)}, device_id_type=MESH
        )

    mixed = (signal_ref[...].astype(F32) * value_ref[...].astype(F32)).astype(BF16)
    row_id = lax.broadcasted_iota(jnp.int32, (2 * width, width), 0)
    col_id = lax.broadcasted_iota(jnp.int32, (2 * width, width), 1)
    target = 2 * own * (col_id // own) + lax.rem(col_id, own)
    pick_signal = (row_id == target).astype(F32).astype(BF16)
    pick_taps = (row_id == target + own).astype(F32).astype(BF16)
    turned = dot(pick_signal, mixed, ((1,), (1,))) + dot(pick_taps, taps_ref[...], ((1,), (1,)))
    out_bf[...] = turned.reshape(groups, 2 * own, rows).astype(BF16)

    pl.semaphore_wait(barrier, groups + chans - 2)

    @pl.loop(1, groups)
    def _(step):
        peer = lax.rem(me + step, groups)
        pltpu.make_async_remote_copy(
            src_ref=out_bf.at[peer],
            dst_ref=in_bf.at[me],
            send_sem=send_sem,
            recv_sem=recv_sem,
            device_id={"seq": peer},
            device_id_type=MESH,
        ).start()

    @pl.loop(1, chans)
    def _(step):
        peer = lax.rem(mine + step, chans)
        pltpu.make_async_remote_copy(
            src_ref=weight_ref.at[pl.ds(peer * width, width)],
            dst_ref=weight_all.at[mine],
            send_sem=weight_send_sem,
            recv_sem=weight_recv_sem,
            device_id={"chan": peer},
            device_id_type=MESH,
        ).start()

    in_bf[pl.ds(me, 1)] = out_bf[pl.ds(me, 1)]
    weight_all[pl.ds(mine, 1)] = weight_ref[pl.ds(mine * width, width)].reshape(1, width, width)
    positions = me * rows + lax.broadcasted_iota(jnp.int32, (rows, starts_ref.shape[1]), 0)
    counted = jnp.sum(
        jnp.where(starts_ref[...] <= positions, 1.0, 0.0).astype(F32), axis=1, keepdims=True
    )
    keep = counted - 2.0 * jnp.floor(0.5 * counted)
    twist_cos = twist_cos_ref[...]
    twist_sin = twist_sin_ref[...]

    whole = in_bf.at[pl.ds(0, groups - 1)]
    pltpu.make_async_copy(whole, whole, recv_sem).wait()

    in_f32[...] = in_bf[...].astype(F32)
    for slot in range(2 * own):
        data = in_f32[:, slot, :].astype(BF16)
        raw = dot(first_hi_ref[...], data) + dot(first_lo_ref[...], data)
        real, imag = raw[:groups], raw[groups:]
        here = pl.ds(slot * groups, groups)
        spec_hi[here, :rows], spec_lo[here, :rows] = halves(real * twist_cos + imag * twist_sin)
        spec_hi[here, rows:], spec_lo[here, rows:] = halves(imag * twist_cos - real * twist_sin)
    spectrum = (
        dot(spec_hi[...], mid_hi_ref[...])
        + dot(spec_lo[...], mid_hi_ref[...])
        + dot(spec_hi[...], mid_lo_ref[...])
    )
    middle = own * groups
    z_re, z_im = spectrum[:middle, :rows], spectrum[:middle, rows:]
    h_re, h_im = spectrum[middle:, :rows], spectrum[middle:, rows:]
    prod_hi, prod_lo = halves(
        jnp.concatenate([z_re * h_re - z_im * h_im, z_re * h_im + z_im * h_re], axis=1)
    )
    inverse = (
        dot(prod_hi, mid_hi_ref[...], ((1,), (1,)))
        + dot(prod_lo, mid_hi_ref[...], ((1,), (1,)))
        + dot(prod_hi, mid_lo_ref[...], ((1,), (1,)))
    )
    for slot in range(own):
        real = inverse[slot * groups : (slot + 1) * groups, :rows]
        imag = inverse[slot * groups : (slot + 1) * groups, rows:]
        high, low = halves(
            jnp.concatenate(
                [real * twist_cos - imag * twist_sin, imag * twist_cos + real * twist_sin], axis=0
            )
        )
        result = (
            dot(last_hi_ref[...], high) + dot(last_hi_ref[...], low) + dot(last_lo_ref[...], high)
        )
        back_f32[:, 2 * slot, :] = result[:, :half]
        back_f32[:, 2 * slot + 1, :] = result[:, half:]
    back_bf[...] = back_f32[...].astype(BF16)

    @pl.loop(1, groups)
    def _(step):
        peer = lax.rem(me + step, groups)
        pltpu.make_async_remote_copy(
            src_ref=back_bf.at[peer],
            dst_ref=home_bf.at[me],
            send_sem=back_send_sem,
            recv_sem=back_recv_sem,
            device_id={"seq": peer},
            device_id_type=MESH,
        ).start()

    home_bf[pl.ds(me, 1)] = back_bf[pl.ds(me, 1)]
    direct = skip_ref[...] * mixed.astype(F32)
    scale = gate_ref[...].astype(F32) * keep
    whole = home_bf.at[pl.ds(0, groups - 1)]
    pltpu.make_async_copy(whole, whole, back_recv_sem).wait()

    home = home_bf[...].astype(F32).reshape(2 * width, half).astype(BF16)
    slot_id = lax.broadcasted_iota(jnp.int32, (2 * width, width), 0)
    chan_id = lax.broadcasted_iota(jnp.int32, (2 * width, width), 1)
    for part in range(2):
        pick = (slot_id == 2 * chan_id + part).astype(F32).astype(BF16)
        conv = dot(home, pick, ((0,), (0,)))
        span = slice(part * half, (part + 1) * half)
        gated = (scale[span] * (conv + direct[span])).astype(BF16)
        gated_all[pl.ds(mine, 1), span, :] = gated.reshape(1, half, width)

    def gated_copy(source, peer, index):
        return pltpu.make_async_remote_copy(
            src_ref=gated_all.at[source],
            dst_ref=gated_all.at[source],
            send_sem=gated_send_sem.at[index],
            recv_sem=gated_recv_sem.at[source],
            device_id={"chan": peer},
            device_id_type=MESH,
        )

    sources = [lax.rem(mine + 2 * step, chans) for step in range(1, chans // 2)]
    sends = [gated_copy(mine, peer, index) for index, peer in enumerate(sources)]
    sends.append(gated_copy(mine, sibling, len(sources)))
    for send in sends:
        send.start()

    whole = weight_all.at[pl.ds(0, chans - 1)]
    pltpu.make_async_copy(whole, whole, weight_recv_sem).wait()

    def term(source):
        return dot(gated_all[source], weight_all[source], ((1,), (1,)))

    def arrived(source):
        block = gated_all.at[source]
        pltpu.make_async_copy(block, block, gated_recv_sem.at[source]).wait()

    total = term(mine)
    order = sorted(range(len(sources)), key=lambda i: min(i + 1, len(sources) - i))
    for i in order:
        arrived(sources[i])
        forward = gated_copy(sources[i], sibling, len(sources) + 1 + i)
        forward.start()
        sends.append(forward)
        total += term(sources[i])
    arrived(sibling)
    total += term(sibling)
    for i in order:
        other = lax.rem(sources[i] + 1, 2) * 1 + (sources[i] - lax.rem(sources[i], 2))
        arrived(other)
        total += term(other)
    out_ref[...] = total.astype(BF16)

    for send in sends:
        send.wait_send()
    for block, sem, count in (
        (in_bf, send_sem, groups - 1),
        (home_bf, back_send_sem, groups - 1),
        (weight_all, weight_send_sem, chans - 1),
    ):
        whole = block.at[pl.ds(0, count)]
        pltpu.make_async_copy(whole, whole, sem).wait()


def on_device(signal_in, value_in, gate_in, filter_taps, skip_gain, turn_starts, out_weight):
    rows, width = signal_in.shape
    groups = lax.axis_size("seq")
    chans = lax.axis_size("chan")
    own = width // groups
    tables = [jnp.asarray(table) for table in make_tables(groups, rows)]
    dma = pltpu.SemaphoreType.DMA
    return pl.pallas_call(
        functools.partial(kernel, groups, chans),
        out_shape=jax.ShapeDtypeStruct((rows, width), BF16),
        in_specs=[pl.BlockSpec(memory_space=pltpu.VMEM)] * (7 + len(tables)),
        out_specs=pl.BlockSpec(memory_space=pltpu.VMEM),
        scratch_shapes=[
            pltpu.VMEM((groups, 2 * own, rows), BF16),
            pltpu.VMEM((groups, 2 * own, rows), BF16),
            pltpu.VMEM((groups, 2 * own, rows), F32),
            pltpu.VMEM((2 * own * groups, 2 * rows), BF16),
            pltpu.VMEM((2 * own * groups, 2 * rows), BF16),
            pltpu.VMEM((groups, 2 * own, rows // 2), F32),
            pltpu.VMEM((groups, 2 * own, rows // 2), BF16),
            pltpu.VMEM((groups, 2 * own, rows // 2), BF16),
            pltpu.VMEM((chans, rows, width), BF16),
            pltpu.VMEM((chans, width, width), BF16),
            dma,
            dma,
            dma,
            dma,
            dma,
            dma,
            dma((chans,)),
            dma((chans,)),
        ],
        compiler_params=pltpu.CompilerParams(collective_id=0, has_side_effects=True),
    )(
        signal_in,
        value_in,
        gate_in,
        filter_taps,
        skip_gain.reshape(1, width),
        turn_starts.reshape(1, -1),
        out_weight,
        *tables,
    )


def solution(mesh):
    in_specs = (
        P("seq", "chan"),
        P("seq", "chan"),
        P("seq", "chan"),
        P("seq", "chan"),
        P("chan"),
        P(),
        P(None, "chan"),
    )
    out_specs = P("seq", "chan")
    return jax.shard_map(
        on_device, mesh=mesh, in_specs=in_specs, out_specs=out_specs, check_vma=False
    )
```

```python
import functools
import math

import jax
import jax.numpy as jnp
import ml_dtypes
import numpy as np
from jax import lax
from jax.experimental import pallas as pl
from jax.experimental.pallas import tpu as pltpu
from jax.sharding import PartitionSpec as P

MESH = pl.DeviceIdType.MESH
F32 = jnp.float32
BF16 = jnp.bfloat16


def split_table(table):
    high = table.astype(ml_dtypes.bfloat16)
    low = (table - high.astype(np.float64)).astype(ml_dtypes.bfloat16)
    return high, low


def make_tables(groups, rows):
    length = 2 * groups * rows
    outer = np.arange(groups)
    inner = np.arange(rows)
    odd = 2 * outer + 1
    angle = 2.0 * math.pi * (odd[:, None] * outer[None, :] % (4 * groups)) / (4 * groups)
    first = np.concatenate([np.cos(angle), -np.sin(angle)], axis=0)
    twist = 2.0 * math.pi * (odd[:, None] * inner[None, :] % (2 * length)) / (2 * length)
    angle = 2.0 * math.pi * (inner[:, None] * inner[None, :] % rows) / rows
    cos, sin = np.cos(angle), np.sin(angle)
    middle = np.block([[cos, -sin], [sin, cos]])
    last = first.T * (2.0 / length)
    return (
        *split_table(first),
        *split_table(last),
        *split_table(middle),
        np.cos(twist).astype(np.float32),
        np.sin(twist).astype(np.float32),
    )


def halves(value):
    high = value.astype(BF16)
    return high, (value - high.astype(F32)).astype(BF16)


def dot(left, right, dims=((1,), (0,))):
    return lax.dot_general(left, right, (dims, ((), ())), preferred_element_type=F32)


def farthest(step, size):
    return lax.rem(size // 2 + (1 - 2 * lax.rem(step, 2)) * ((step + 1) // 2), size)


def kernel(
    groups,
    chans,
    signal_ref,
    value_ref,
    gate_ref,
    taps_ref,
    skip_ref,
    starts_ref,
    weight_ref,
    first_hi_ref,
    first_lo_ref,
    last_hi_ref,
    last_lo_ref,
    mid_hi_ref,
    mid_lo_ref,
    twist_cos_ref,
    twist_sin_ref,
    out_ref,
    out_bf,
    in_bf,
    in_f32,
    spec_hi,
    spec_lo,
    back_f32,
    back_bf,
    home_bf,
    gated_all,
    weight_all,
    passing,
    mid_hi,
    mid_lo,
    load_sem,
    first_send_sem,
    first_recv_sem,
    send_sem,
    recv_sem,
    back_send_sem,
    back_recv_sem,
    weight_send_sem,
    weight_recv_sem,
    gated_send_sem,
    gated_recv_sem,
):
    rows, width = signal_ref.shape
    own = width // groups
    half = rows // 2
    side = math.isqrt(groups)
    me = lax.axis_index("seq")
    mine = lax.axis_index("chan")
    row, col = me // side, lax.rem(me, side)
    core = lax.rem(mine, 2)
    sibling = mine + 1 - 2 * core

    def along_row(step):
        return lax.rem(col + farthest(step, side), side)

    def along_col(step):
        return lax.rem(row + farthest(step, side), side)

    barrier = pltpu.get_barrier_semaphore()

    @pl.loop(0, side - 1)
    def _(step):
        for peer in (along_col(step) * side + col, row * side + along_row(step)):
            pl.semaphore_signal(barrier, inc=1, device_id={"seq": peer}, device_id_type=MESH)

    @pl.loop(1, chans)
    def _(step):
        pl.semaphore_signal(
            barrier, inc=1, device_id={"chan": lax.rem(mine + step, chans)}, device_id_type=MESH
        )

    loads = [
        pltpu.make_async_copy(mid_hi_ref, mid_hi, load_sem.at[0]),
        pltpu.make_async_copy(mid_lo_ref, mid_lo, load_sem.at[1]),
        pltpu.make_async_copy(
            weight_ref.at[pl.ds(mine * width, width)], weight_all.at[mine], load_sem.at[2]
        ),
    ]
    for load in loads:
        load.start()

    mixed = (signal_ref[...].astype(F32) * value_ref[...].astype(F32)).astype(BF16)
    row_id = lax.broadcasted_iota(jnp.int32, (2 * width, width), 0)
    col_id = lax.broadcasted_iota(jnp.int32, (2 * width, width), 1)
    target = 2 * own * (col_id // own) + lax.rem(col_id, own)
    pick_signal = (row_id == target).astype(F32).astype(BF16)
    pick_taps = (row_id == target + own).astype(F32).astype(BF16)
    turned = dot(pick_signal, mixed, ((1,), (1,))) + dot(pick_taps, taps_ref[...], ((1,), (1,)))
    out_bf[...] = turned.reshape(side, side, 2 * own, rows).astype(BF16)

    pl.semaphore_wait(barrier, 2 * (side - 1) + chans - 1)

    @pl.loop(0, side - 1)
    def _(step):
        peer = along_col(step)
        pltpu.make_async_remote_copy(
            src_ref=out_bf.at[peer],
            dst_ref=passing.at[row],
            send_sem=first_send_sem,
            recv_sem=first_recv_sem.at[row],
            device_id={"seq": peer * side + col},
            device_id_type=MESH,
        ).start()

    def pass_on(block, source):
        @pl.loop(0, side - 1)
        def _(step):
            peer = along_row(step)
            pltpu.make_async_remote_copy(
                src_ref=block.at[source, peer],
                dst_ref=in_bf.at[source, col],
                send_sem=send_sem,
                recv_sem=recv_sem,
                device_id={"seq": row * side + peer},
                device_id_type=MESH,
            ).start()

        in_bf[pl.ds(source, 1), pl.ds(col, 1)] = block[pl.ds(source, 1), pl.ds(col, 1)]

    pass_on(out_bf, row)

    @pl.loop(1, chans)
    def _(step):
        peer = lax.rem(mine + step, chans)
        pltpu.make_async_remote_copy(
            src_ref=weight_ref.at[pl.ds(peer * width, width)],
            dst_ref=weight_all.at[mine],
            send_sem=weight_send_sem,
            recv_sem=weight_recv_sem,
            device_id={"chan": peer},
            device_id_type=MESH,
        ).start()

    @pl.loop(0, side - 1)
    def _(step):
        source = along_col(step)
        block = passing.at[source]
        pltpu.make_async_copy(block, block, first_recv_sem.at[source]).wait()
        pass_on(passing, source)

    positions = me * rows + lax.broadcasted_iota(jnp.int32, (rows, starts_ref.shape[1]), 0)
    counted = jnp.sum(
        jnp.where(starts_ref[...] <= positions, 1.0, 0.0).astype(F32), axis=1, keepdims=True
    )
    keep = counted - 2.0 * jnp.floor(0.5 * counted)
    twist_cos = twist_cos_ref[...]
    twist_sin = twist_sin_ref[...]

    whole = in_bf.at[pl.ds(0, side - 1)]
    pltpu.make_async_copy(whole, whole, recv_sem).wait()
    for load in loads:
        load.wait()

    in_f32[...] = in_bf[...].astype(F32).reshape(groups, 2 * own, rows)
    for slot in range(2 * own):
        data = in_f32[:, slot, :].astype(BF16)
        raw = dot(first_hi_ref[...], data) + dot(first_lo_ref[...], data)
        real, imag = raw[:groups], raw[groups:]
        here = pl.ds(slot * groups, groups)
        spec_hi[here, :rows], spec_lo[here, :rows] = halves(real * twist_cos + imag * twist_sin)
        spec_hi[here, rows:], spec_lo[here, rows:] = halves(imag * twist_cos - real * twist_sin)
    spectrum = (
        dot(spec_hi[...], mid_hi[...])
        + dot(spec_lo[...], mid_hi[...])
        + dot(spec_hi[...], mid_lo[...])
    )
    middle = own * groups
    z_re, z_im = spectrum[:middle, :rows], spectrum[:middle, rows:]
    h_re, h_im = spectrum[middle:, :rows], spectrum[middle:, rows:]
    prod_hi, prod_lo = halves(
        jnp.concatenate([z_re * h_re - z_im * h_im, z_re * h_im + z_im * h_re], axis=1)
    )
    inverse = (
        dot(prod_hi, mid_hi[...], ((1,), (1,)))
        + dot(prod_lo, mid_hi[...], ((1,), (1,)))
        + dot(prod_hi, mid_lo[...], ((1,), (1,)))
    )
    for slot in range(own):
        real = inverse[slot * groups : (slot + 1) * groups, :rows]
        imag = inverse[slot * groups : (slot + 1) * groups, rows:]
        high, low = halves(
            jnp.concatenate(
                [real * twist_cos - imag * twist_sin, imag * twist_cos + real * twist_sin], axis=0
            )
        )
        result = (
            dot(last_hi_ref[...], high) + dot(last_hi_ref[...], low) + dot(last_lo_ref[...], high)
        )
        back_f32[:, 2 * slot, :] = result[:, :half]
        back_f32[:, 2 * slot + 1, :] = result[:, half:]
    back_bf[...] = back_f32[...].astype(BF16)

    @pl.loop(0, groups - 1)
    def _(step):
        peer = along_col(step // side) * side + along_row(lax.rem(step, side))
        pltpu.make_async_remote_copy(
            src_ref=back_bf.at[peer],
            dst_ref=home_bf.at[me],
            send_sem=back_send_sem,
            recv_sem=back_recv_sem,
            device_id={"seq": peer},
            device_id_type=MESH,
        ).start()

    home_bf[pl.ds(me, 1)] = back_bf[pl.ds(me, 1)]
    direct = skip_ref[...] * mixed.astype(F32)
    scale = gate_ref[...].astype(F32) * keep
    whole = home_bf.at[pl.ds(0, groups - 1)]
    pltpu.make_async_copy(whole, whole, back_recv_sem).wait()

    home = home_bf[...].astype(F32).reshape(2 * width, half).astype(BF16)
    slot_id = lax.broadcasted_iota(jnp.int32, (2 * width, width), 0)
    chan_id = lax.broadcasted_iota(jnp.int32, (2 * width, width), 1)
    for part in range(2):
        pick = (slot_id == 2 * chan_id + part).astype(F32).astype(BF16)
        conv = dot(home, pick, ((0,), (0,)))
        span = slice(part * half, (part + 1) * half)
        gated = (scale[span] * (conv + direct[span])).astype(BF16)
        gated_all[pl.ds(mine, 1), span, :] = gated.reshape(1, half, width)

    sends = []

    def gated_copy(source, part, peer):
        block = gated_all.at[source, pl.ds(part * half, half)]
        copy = pltpu.make_async_remote_copy(
            src_ref=block,
            dst_ref=block,
            send_sem=gated_send_sem.at[len(sends)],
            recv_sem=gated_recv_sem.at[source, part],
            device_id={"chan": peer},
            device_id_type=MESH,
        )
        copy.start()
        sends.append(copy)

    def arrived(source, part):
        block = gated_all.at[source, pl.ds(part * half, half)]
        pltpu.make_async_copy(block, block, gated_recv_sem.at[source, part]).wait()

    right, far, left = [lax.rem(mine + 2 * step, chans) for step in (1, 2, 3)]
    for part in range(2):
        gated_copy(mine, part, right)
        gated_copy(mine, 1 - part, left)
    for part in range(2):
        gated_copy(mine, part, sibling)

    whole = weight_all.at[pl.ds(0, chans - 1)]
    pltpu.make_async_copy(whole, whole, weight_recv_sem).wait()

    def term(source):
        return dot(gated_all[source], weight_all[source], ((1,), (1,)))

    total = term(mine)
    for source, part, onward in ((left, 0, right), (right, 1, left)):
        arrived(source, part)
        gated_copy(source, part, onward)
        gated_copy(source, part, sibling)
    for source, part in ((left, 1), (right, 0)):
        arrived(source, part)
        gated_copy(source, part, sibling)
        total += term(source)
    arrived(sibling, 0)
    arrived(sibling, 1)
    total += term(sibling)
    for part in range(2):
        arrived(far, part)
        gated_copy(far, part, sibling)
    total += term(far)
    for source in (left, right, far):
        other = source + 1 - 2 * core
        arrived(other, 0)
        arrived(other, 1)
        total += term(other)
    out_ref[...] = total.astype(BF16)

    for send in sends:
        send.wait_send()
    for block, sem, count in (
        (passing, first_send_sem, side - 1),
        (in_bf, send_sem, side - 1),
        (home_bf, back_send_sem, groups - 1),
        (weight_all, weight_send_sem, chans - 1),
    ):
        whole = block.at[pl.ds(0, count)]
        pltpu.make_async_copy(whole, whole, sem).wait()


def on_device(signal_in, value_in, gate_in, filter_taps, skip_gain, turn_starts, out_weight):
    rows, width = signal_in.shape
    groups = lax.axis_size("seq")
    chans = lax.axis_size("chan")
    own = width // groups
    side = math.isqrt(groups)
    tables = [jnp.asarray(table) for table in make_tables(groups, rows)]
    dma = pltpu.SemaphoreType.DMA
    return pl.pallas_call(
        functools.partial(kernel, groups, chans),
        out_shape=jax.ShapeDtypeStruct((rows, width), BF16),
        in_specs=[
            pl.BlockSpec(memory_space=pl.ANY if place in (6, 11, 12) else pltpu.VMEM)
            for place in range(7 + len(tables))
        ],
        out_specs=pl.BlockSpec(memory_space=pltpu.VMEM),
        scratch_shapes=[
            pltpu.VMEM((side, side, 2 * own, rows), BF16),
            pltpu.VMEM((side, side, 2 * own, rows), BF16),
            pltpu.VMEM((groups, 2 * own, rows), F32),
            pltpu.VMEM((2 * own * groups, 2 * rows), BF16),
            pltpu.VMEM((2 * own * groups, 2 * rows), BF16),
            pltpu.VMEM((groups, 2 * own, rows // 2), F32),
            pltpu.VMEM((groups, 2 * own, rows // 2), BF16),
            pltpu.VMEM((groups, 2 * own, rows // 2), BF16),
            pltpu.VMEM((chans, rows, width), BF16),
            pltpu.VMEM((chans, width, width), BF16),
            pltpu.VMEM((side, side, 2 * own, rows), BF16),
            pltpu.VMEM((2 * rows, 2 * rows), BF16),
            pltpu.VMEM((2 * rows, 2 * rows), BF16),
            dma((3,)),
            dma,
            dma((side,)),
            dma,
            dma,
            dma,
            dma,
            dma,
            dma,
            dma((14,)),
            dma((chans, 2)),
        ],
        compiler_params=pltpu.CompilerParams(collective_id=0, has_side_effects=True),
    )(
        signal_in,
        value_in,
        gate_in,
        filter_taps,
        skip_gain.reshape(1, width),
        turn_starts.reshape(1, -1),
        out_weight,
        *tables,
    )


def solution(mesh):
    in_specs = (
        P("seq", "chan"),
        P("seq", "chan"),
        P("seq", "chan"),
        P("seq", "chan"),
        P("chan"),
        P(),
        P(None, "chan"),
    )
    out_specs = P("seq", "chan")
    return jax.shard_map(
        on_device, mesh=mesh, in_specs=in_specs, out_specs=out_specs, check_vma=False
    )
```

```python
import functools
import math

import jax
import jax.numpy as jnp
import ml_dtypes
import numpy as np
from jax import lax
from jax.experimental import pallas as pl
from jax.experimental.pallas import tpu as pltpu
from jax.sharding import PartitionSpec as P

PIECES = 2
MESH = pl.DeviceIdType.MESH
F32 = jnp.float32
BF16 = jnp.bfloat16


def split_table(table):
    high = table.astype(ml_dtypes.bfloat16)
    low = (table - high.astype(np.float64)).astype(ml_dtypes.bfloat16)
    return high, low


def make_tables(groups, rows):
    length = 2 * groups * rows
    outer = np.arange(groups)
    inner = np.arange(rows)
    odd = 2 * outer + 1
    angle = 2.0 * math.pi * (odd[:, None] * outer[None, :] % (4 * groups)) / (4 * groups)
    first = np.concatenate([np.cos(angle), -np.sin(angle)], axis=0)
    twist = 2.0 * math.pi * (odd[:, None] * inner[None, :] % (2 * length)) / (2 * length)
    angle = 2.0 * math.pi * (inner[:, None] * inner[None, :] % rows) / rows
    cos, sin = np.cos(angle), np.sin(angle)
    middle = np.block([[cos, -sin], [sin, cos]])
    last = first.T * (2.0 / length)
    return (
        *split_table(first),
        *split_table(last),
        *split_table(middle),
        np.cos(twist).astype(np.float32),
        np.sin(twist).astype(np.float32),
    )


def halves(value):
    high = value.astype(BF16)
    return high, (value - high.astype(F32)).astype(BF16)


def dot(left, right, dims=((1,), (0,))):
    return lax.dot_general(left, right, (dims, ((), ())), preferred_element_type=F32)


def farthest(step, size):
    return lax.rem(size // 2 + (1 - 2 * lax.rem(step, 2)) * ((step + 1) // 2), size)


def kernel(
    groups,
    chans,
    signal_hbm,
    value_hbm,
    gate_hbm,
    taps_hbm,
    skip_hbm,
    starts_hbm,
    weight_ref,
    first_hi_hbm,
    first_lo_hbm,
    last_hi_hbm,
    last_lo_hbm,
    mid_hi_hbm,
    mid_lo_hbm,
    twist_cos_hbm,
    twist_sin_hbm,
    out_ref,
    out_bf,
    in_bf,
    in_f32,
    spec_hi,
    spec_lo,
    back_f32,
    back_bf,
    home_bf,
    gated_all,
    weight_all,
    signal_ref,
    value_ref,
    gate_ref,
    taps_ref,
    skip_ref,
    starts_ref,
    first_hi_ref,
    first_lo_ref,
    last_hi_ref,
    last_lo_ref,
    mid_hi_ref,
    mid_lo_ref,
    twist_cos_ref,
    twist_sin_ref,
    load_sem,
    send_sem,
    recv_sem,
    back_send_sem,
    back_recv_sem,
    weight_send_sem,
    weight_recv_sem,
    gated_send_sem,
    gated_recv_sem,
):
    rows, width = signal_hbm.shape
    own = width // groups
    half = rows // 2
    side = math.isqrt(groups)
    me = lax.axis_index("seq")
    mine = lax.axis_index("chan")
    row, col = me // side, lax.rem(me, side)
    core = lax.rem(mine, 2)
    sibling = mine + 1 - 2 * core

    def along_row(step):
        return lax.rem(col + farthest(step, side), side)

    def along_col(step):
        return lax.rem(row + farthest(step, side), side)

    def peer_of(step):
        return along_col(step // side) * side + along_row(lax.rem(step, side))

    barrier = pltpu.get_barrier_semaphore()

    @pl.loop(0, groups - 1)
    def _(step):
        pl.semaphore_signal(
            barrier, inc=1, device_id={"seq": peer_of(step)}, device_id_type=MESH
        )

    @pl.loop(1, chans)
    def _(step):
        pl.semaphore_signal(
            barrier, inc=1, device_id={"chan": lax.rem(mine + step, chans)}, device_id_type=MESH
        )

    held = (
        (signal_hbm, signal_ref),
        (value_hbm, value_ref),
        (gate_hbm, gate_ref),
        (taps_hbm, taps_ref),
        (skip_hbm, skip_ref),
        (starts_hbm, starts_ref),
        (first_hi_hbm, first_hi_ref),
        (first_lo_hbm, first_lo_ref),
        (last_hi_hbm, last_hi_ref),
        (last_lo_hbm, last_lo_ref),
        (mid_hi_hbm, mid_hi_ref),
        (mid_lo_hbm, mid_lo_ref),
        (twist_cos_hbm, twist_cos_ref),
        (twist_sin_hbm, twist_sin_ref),
    )
    loads = [
        pltpu.make_async_copy(source, target, load_sem.at[place])
        for place, (source, target) in enumerate(held)
    ]
    loads.append(
        pltpu.make_async_copy(
            weight_ref.at[pl.ds(mine * width, width)], weight_all.at[mine], load_sem.at[len(held)]
        )
    )
    for load in loads:
        load.start()
    for place in (0, 1, 3):
        loads[place].wait()

    mixed = (signal_ref[...].astype(F32) * value_ref[...].astype(F32)).astype(BF16)
    row_id = lax.broadcasted_iota(jnp.int32, (2 * width, width), 0)
    col_id = lax.broadcasted_iota(jnp.int32, (2 * width, width), 1)
    target = 2 * own * (col_id // own) + lax.rem(col_id, own)
    pick_signal = (row_id == target).astype(F32).astype(BF16)
    pick_taps = (row_id == target + own).astype(F32).astype(BF16)
    turned = dot(pick_signal, mixed, ((1,), (1,))) + dot(pick_taps, taps_ref[...], ((1,), (1,)))
    out_bf[...] = turned.reshape(groups, 2 * own, rows).astype(BF16)

    pl.semaphore_wait(barrier, groups + chans - 2)

    @pl.loop(0, groups - 1)
    def _(step):
        peer = peer_of(step)
        pltpu.make_async_remote_copy(
            src_ref=out_bf.at[peer],
            dst_ref=in_bf.at[me],
            send_sem=send_sem,
            recv_sem=recv_sem,
            device_id={"seq": peer},
            device_id_type=MESH,
        ).start()

    @pl.loop(1, chans)
    def _(step):
        peer = lax.rem(mine + step, chans)
        pltpu.make_async_remote_copy(
            src_ref=weight_ref.at[pl.ds(peer * width, width)],
            dst_ref=weight_all.at[mine],
            send_sem=weight_send_sem,
            recv_sem=weight_recv_sem,
            device_id={"chan": peer},
            device_id_type=MESH,
        ).start()

    in_bf[pl.ds(me, 1)] = out_bf[pl.ds(me, 1)]
    for place in (2, *range(4, len(loads))):
        loads[place].wait()
    positions = me * rows + lax.broadcasted_iota(jnp.int32, (rows, starts_ref.shape[1]), 0)
    counted = jnp.sum(
        jnp.where(starts_ref[...] <= positions, 1.0, 0.0).astype(F32), axis=1, keepdims=True
    )
    keep = counted - 2.0 * jnp.floor(0.5 * counted)
    twist_cos = twist_cos_ref[...]
    twist_sin = twist_sin_ref[...]

    whole = in_bf.at[pl.ds(0, groups - 1)]
    pltpu.make_async_copy(whole, whole, recv_sem).wait()

    in_f32[...] = in_bf[...].astype(F32)
    for slot in range(2 * own):
        data = in_f32[:, slot, :].astype(BF16)
        raw = dot(first_hi_ref[...], data) + dot(first_lo_ref[...], data)
        real, imag = raw[:groups], raw[groups:]
        here = pl.ds(slot * groups, groups)
        spec_hi[here, :rows], spec_lo[here, :rows] = halves(real * twist_cos + imag * twist_sin)
        spec_hi[here, rows:], spec_lo[here, rows:] = halves(imag * twist_cos - real * twist_sin)
    spectrum = (
        dot(spec_hi[...], mid_hi_ref[...])
        + dot(spec_lo[...], mid_hi_ref[...])
        + dot(spec_hi[...], mid_lo_ref[...])
    )
    middle = own * groups
    z_re, z_im = spectrum[:middle, :rows], spectrum[:middle, rows:]
    h_re, h_im = spectrum[middle:, :rows], spectrum[middle:, rows:]
    prod_hi, prod_lo = halves(
        jnp.concatenate([z_re * h_re - z_im * h_im, z_re * h_im + z_im * h_re], axis=1)
    )
    inverse = (
        dot(prod_hi, mid_hi_ref[...], ((1,), (1,)))
        + dot(prod_lo, mid_hi_ref[...], ((1,), (1,)))
        + dot(prod_hi, mid_lo_ref[...], ((1,), (1,)))
    )
    for slot in range(own):
        real = inverse[slot * groups : (slot + 1) * groups, :rows]
        imag = inverse[slot * groups : (slot + 1) * groups, rows:]
        high, low = halves(
            jnp.concatenate(
                [real * twist_cos - imag * twist_sin, imag * twist_cos + real * twist_sin], axis=0
            )
        )
        result = (
            dot(last_hi_ref[...], high) + dot(last_hi_ref[...], low) + dot(last_lo_ref[...], high)
        )
        back_f32[:, 2 * slot, :] = result[:, :half]
        back_f32[:, 2 * slot + 1, :] = result[:, half:]
    back_bf[...] = back_f32[...].astype(BF16)

    @pl.loop(0, groups - 1)
    def _(step):
        peer = peer_of(step)
        pltpu.make_async_remote_copy(
            src_ref=back_bf.at[peer],
            dst_ref=home_bf.at[me],
            send_sem=back_send_sem,
            recv_sem=back_recv_sem,
            device_id={"seq": peer},
            device_id_type=MESH,
        ).start()

    home_bf[pl.ds(me, 1)] = back_bf[pl.ds(me, 1)]
    direct = skip_ref[...] * mixed.astype(F32)
    scale = gate_ref[...].astype(F32) * keep
    whole = home_bf.at[pl.ds(0, groups - 1)]
    pltpu.make_async_copy(whole, whole, back_recv_sem).wait()

    home = home_bf[...].astype(F32).reshape(2 * width, half).astype(BF16)
    slot_id = lax.broadcasted_iota(jnp.int32, (2 * width, width), 0)
    chan_id = lax.broadcasted_iota(jnp.int32, (2 * width, width), 1)
    for part in range(2):
        pick = (slot_id == 2 * chan_id + part).astype(F32).astype(BF16)
        conv = dot(home, pick, ((0,), (0,)))
        span = slice(part * half, (part + 1) * half)
        gated = (scale[span] * (conv + direct[span])).astype(BF16)
        gated_all[pl.ds(mine, 1), span, :] = gated.reshape(1, half, width)

    sends = []
    piece = rows // PIECES

    def gated_copy(source, part, peer):
        block = gated_all.at[source, pl.ds(part * piece, piece)]
        copy = pltpu.make_async_remote_copy(
            src_ref=block,
            dst_ref=block,
            send_sem=gated_send_sem.at[len(sends)],
            recv_sem=gated_recv_sem.at[source, part],
            device_id={"chan": peer},
            device_id_type=MESH,
        )
        copy.start()
        sends.append(copy)

    def arrived(source, part):
        block = gated_all.at[source, pl.ds(part * piece, piece)]
        pltpu.make_async_copy(block, block, gated_recv_sem.at[source, part]).wait()

    right, far, left = [lax.rem(mine + 2 * step, chans) for step in (1, 2, 3)]
    via, back = left, right
    gated_copy(mine, 1, via)
    gated_copy(mine, 0, far)
    gated_copy(mine, 0, via)
    gated_copy(mine, 0, back)
    gated_copy(mine, 1, back)
    for part in range(PIECES):
        gated_copy(mine, part, sibling)

    whole = weight_all.at[pl.ds(0, chans - 1)]
    pltpu.make_async_copy(whole, whole, weight_recv_sem).wait()

    def term(source):
        return dot(gated_all[source], weight_all[source], ((1,), (1,)))

    total = term(mine)
    for part in range(PIECES):
        arrived(sibling, part)
    total += term(sibling)
    arrived(back, 1)
    gated_copy(back, 1, via)
    gated_copy(back, 1, sibling)
    for source, part in ((back, 0), (via, 0), (far, 0), (via, 1), (far, 1)):
        arrived(source, part)
        gated_copy(source, part, sibling)
    for source in (far, left, right):
        total += term(source)
    for source in (far, left, right):
        other = source + 1 - 2 * core
        for part in range(PIECES):
            arrived(other, part)
        total += term(other)
    out_ref[...] = total.astype(BF16)

    for send in sends:
        send.wait_send()
    for block, sem, count in (
        (in_bf, send_sem, groups - 1),
        (home_bf, back_send_sem, groups - 1),
        (weight_all, weight_send_sem, chans - 1),
    ):
        whole = block.at[pl.ds(0, count)]
        pltpu.make_async_copy(whole, whole, sem).wait()


def on_device(signal_in, value_in, gate_in, filter_taps, skip_gain, turn_starts, out_weight):
    rows, width = signal_in.shape
    groups = lax.axis_size("seq")
    chans = lax.axis_size("chan")
    own = width // groups
    tables = [jnp.asarray(table) for table in make_tables(groups, rows)]
    held = (
        signal_in,
        value_in,
        gate_in,
        filter_taps,
        skip_gain.reshape(1, width),
        turn_starts.reshape(1, -1),
        *tables,
    )
    dma = pltpu.SemaphoreType.DMA
    return pl.pallas_call(
        functools.partial(kernel, groups, chans),
        out_shape=jax.ShapeDtypeStruct((rows, width), BF16),
        in_specs=[pl.BlockSpec(memory_space=pl.ANY)] * (7 + len(tables)),
        out_specs=pl.BlockSpec(memory_space=pltpu.VMEM),
        scratch_shapes=[
            pltpu.VMEM((groups, 2 * own, rows), BF16),
            pltpu.VMEM((groups, 2 * own, rows), BF16),
            pltpu.VMEM((groups, 2 * own, rows), F32),
            pltpu.VMEM((2 * own * groups, 2 * rows), BF16),
            pltpu.VMEM((2 * own * groups, 2 * rows), BF16),
            pltpu.VMEM((groups, 2 * own, rows // 2), F32),
            pltpu.VMEM((groups, 2 * own, rows // 2), BF16),
            pltpu.VMEM((groups, 2 * own, rows // 2), BF16),
            pltpu.VMEM((chans, rows, width), BF16),
            pltpu.VMEM((chans, width, width), BF16),
            *[pltpu.VMEM(array.shape, array.dtype) for array in held],
            dma((len(held) + 1,)),
            dma,
            dma,
            dma,
            dma,
            dma,
            dma,
            dma((7 * PIECES,)),
            dma((chans, PIECES)),
        ],
        compiler_params=pltpu.CompilerParams(collective_id=0, has_side_effects=True),
    )(*held[:6], out_weight, *held[6:])


def solution(mesh):
    in_specs = (
        P("seq", "chan"),
        P("seq", "chan"),
        P("seq", "chan"),
        P("seq", "chan"),
        P("chan"),
        P(),
        P(None, "chan"),
    )
    out_specs = P("seq", "chan")
    return jax.shard_map(
        on_device, mesh=mesh, in_specs=in_specs, out_specs=out_specs, check_vma=False
    )
```

```python
import functools
import math

import jax
import jax.numpy as jnp
import ml_dtypes
import numpy as np
from jax import lax
from jax.experimental import pallas as pl
from jax.experimental.pallas import tpu as pltpu
from jax.sharding import PartitionSpec as P

PIECES = 2
MESH = pl.DeviceIdType.MESH
F32 = jnp.float32
BF16 = jnp.bfloat16


def split_table(table):
    high = table.astype(ml_dtypes.bfloat16)
    low = (table - high.astype(np.float64)).astype(ml_dtypes.bfloat16)
    return high, low


def make_tables(groups, rows):
    length = 2 * groups * rows
    outer = np.arange(groups)
    inner = np.arange(rows)
    odd = 2 * outer + 1
    angle = 2.0 * math.pi * (odd[:, None] * outer[None, :] % (4 * groups)) / (4 * groups)
    first = np.concatenate([np.cos(angle), -np.sin(angle)], axis=0)
    twist = 2.0 * math.pi * (odd[:, None] * inner[None, :] % (2 * length)) / (2 * length)
    angle = 2.0 * math.pi * (inner[:, None] * inner[None, :] % rows) / rows
    cos, sin = np.cos(angle), np.sin(angle)
    middle = np.block([[cos, -sin], [sin, cos]])
    last = first.T * (2.0 / length)
    return (
        *split_table(first),
        *split_table(last),
        *split_table(middle),
        np.cos(twist).astype(np.float32),
        np.sin(twist).astype(np.float32),
    )


def halves(value):
    high = value.astype(BF16)
    return high, (value - high.astype(F32)).astype(BF16)


def dot(left, right, dims=((1,), (0,))):
    return lax.dot_general(left, right, (dims, ((), ())), preferred_element_type=F32)


def farthest(step, size):
    return (size // 2 + (1 - 2 * (step % 2)) * ((step + 1) // 2)) % size


def kernel(
    groups,
    chans,
    signal_hbm,
    value_hbm,
    gate_hbm,
    taps_hbm,
    skip_hbm,
    starts_hbm,
    weight_ref,
    first_hi_hbm,
    first_lo_hbm,
    last_hi_hbm,
    last_lo_hbm,
    mid_hi_hbm,
    mid_lo_hbm,
    twist_cos_hbm,
    twist_sin_hbm,
    out_ref,
    out_bf,
    in_bf,
    in_f32,
    spec_hi,
    spec_lo,
    back_f32,
    back_bf,
    home_bf,
    gated_all,
    weight_all,
    signal_ref,
    value_ref,
    gate_ref,
    taps_ref,
    skip_ref,
    starts_ref,
    first_hi_ref,
    first_lo_ref,
    last_hi_ref,
    last_lo_ref,
    mid_hi_ref,
    mid_lo_ref,
    twist_cos_ref,
    twist_sin_ref,
    load_sem,
    send_sem,
    recv_sem,
    back_send_sem,
    back_recv_sem,
    weight_send_sem,
    weight_recv_sem,
    gated_send_sem,
    gated_recv_sem,
):
    rows, width = signal_hbm.shape
    own = width // groups
    half = rows // 2
    side = math.isqrt(groups)
    me = lax.axis_index("seq")
    mine = lax.axis_index("chan")
    row, col = me // side, lax.rem(me, side)
    core = lax.rem(mine, 2)
    sibling = mine + 1 - 2 * core

    cols = [lax.rem(col + farthest(step, side), side) for step in range(side)]

    def for_peers(act):
        @pl.loop(0, side - 1)
        def _(step):
            offset = side // 2 + (1 - 2 * lax.rem(step, 2)) * ((step + 1) // 2)
            base = lax.rem(row + offset, side) * side
            for other in cols:
                act(base + other)

        for other in cols[:-1]:
            act(row * side + other)

    barrier = pltpu.get_barrier_semaphore()

    @for_peers
    def _(peer):
        pl.semaphore_signal(barrier, inc=1, device_id={"seq": peer}, device_id_type=MESH)

    @pl.loop(1, chans)
    def _(step):
        pl.semaphore_signal(
            barrier, inc=1, device_id={"chan": lax.rem(mine + step, chans)}, device_id_type=MESH
        )

    held = (
        (signal_hbm, signal_ref),
        (value_hbm, value_ref),
        (gate_hbm, gate_ref),
        (taps_hbm, taps_ref),
        (skip_hbm, skip_ref),
        (starts_hbm, starts_ref),
        (first_hi_hbm, first_hi_ref),
        (first_lo_hbm, first_lo_ref),
        (last_hi_hbm, last_hi_ref),
        (last_lo_hbm, last_lo_ref),
        (mid_hi_hbm, mid_hi_ref),
        (mid_lo_hbm, mid_lo_ref),
        (twist_cos_hbm, twist_cos_ref),
        (twist_sin_hbm, twist_sin_ref),
    )
    loads = [
        pltpu.make_async_copy(source, target, load_sem.at[place])
        for place, (source, target) in enumerate(held)
    ]
    loads.append(
        pltpu.make_async_copy(
            weight_ref.at[pl.ds(mine * width, width)], weight_all.at[mine], load_sem.at[len(held)]
        )
    )
    for load in loads:
        load.start()
    for place in (0, 1, 3):
        loads[place].wait()

    mixed = (signal_ref[...].astype(F32) * value_ref[...].astype(F32)).astype(BF16)
    row_id = lax.broadcasted_iota(jnp.int32, (2 * width, width), 0)
    col_id = lax.broadcasted_iota(jnp.int32, (2 * width, width), 1)
    target = 2 * own * (col_id // own) + lax.rem(col_id, own)
    pick_signal = (row_id == target).astype(F32).astype(BF16)
    pick_taps = (row_id == target + own).astype(F32).astype(BF16)
    turned = dot(pick_signal, mixed, ((1,), (1,))) + dot(pick_taps, taps_ref[...], ((1,), (1,)))
    out_bf[...] = turned.reshape(groups, 2 * own, rows).astype(BF16)

    pl.semaphore_wait(barrier, groups + chans - 2)

    @for_peers
    def _(peer):
        pltpu.make_async_remote_copy(
            src_ref=out_bf.at[peer],
            dst_ref=in_bf.at[me],
            send_sem=send_sem,
            recv_sem=recv_sem,
            device_id={"seq": peer},
            device_id_type=MESH,
        ).start()

    @pl.loop(1, chans)
    def _(step):
        peer = lax.rem(mine + step, chans)
        pltpu.make_async_remote_copy(
            src_ref=weight_ref.at[pl.ds(peer * width, width)],
            dst_ref=weight_all.at[mine],
            send_sem=weight_send_sem,
            recv_sem=weight_recv_sem,
            device_id={"chan": peer},
            device_id_type=MESH,
        ).start()

    in_bf[pl.ds(me, 1)] = out_bf[pl.ds(me, 1)]
    for place in (2, *range(4, len(loads))):
        loads[place].wait()
    positions = me * rows + lax.broadcasted_iota(jnp.int32, (rows, starts_ref.shape[1]), 0)
    counted = jnp.sum(
        jnp.where(starts_ref[...] <= positions, 1.0, 0.0).astype(F32), axis=1, keepdims=True
    )
    keep = counted - 2.0 * jnp.floor(0.5 * counted)
    twist_cos = twist_cos_ref[...]
    twist_sin = twist_sin_ref[...]

    whole = in_bf.at[pl.ds(0, groups - 1)]
    pltpu.make_async_copy(whole, whole, recv_sem).wait()

    in_f32[...] = in_bf[...].astype(F32)
    for slot in range(2 * own):
        data = in_f32[:, slot, :].astype(BF16)
        raw = dot(first_hi_ref[...], data) + dot(first_lo_ref[...], data)
        real, imag = raw[:groups], raw[groups:]
        here = pl.ds(slot * groups, groups)
        spec_hi[here, :rows], spec_lo[here, :rows] = halves(real * twist_cos + imag * twist_sin)
        spec_hi[here, rows:], spec_lo[here, rows:] = halves(imag * twist_cos - real * twist_sin)
    spectrum = (
        dot(spec_hi[...], mid_hi_ref[...])
        + dot(spec_lo[...], mid_hi_ref[...])
        + dot(spec_hi[...], mid_lo_ref[...])
    )
    middle = own * groups
    z_re, z_im = spectrum[:middle, :rows], spectrum[:middle, rows:]
    h_re, h_im = spectrum[middle:, :rows], spectrum[middle:, rows:]
    prod_hi, prod_lo = halves(
        jnp.concatenate([z_re * h_re - z_im * h_im, z_re * h_im + z_im * h_re], axis=1)
    )
    inverse = (
        dot(prod_hi, mid_hi_ref[...], ((1,), (1,)))
        + dot(prod_lo, mid_hi_ref[...], ((1,), (1,)))
        + dot(prod_hi, mid_lo_ref[...], ((1,), (1,)))
    )
    for slot in range(own):
        real = inverse[slot * groups : (slot + 1) * groups, :rows]
        imag = inverse[slot * groups : (slot + 1) * groups, rows:]
        high, low = halves(
            jnp.concatenate(
                [real * twist_cos - imag * twist_sin, imag * twist_cos + real * twist_sin], axis=0
            )
        )
        result = (
            dot(last_hi_ref[...], high) + dot(last_hi_ref[...], low) + dot(last_lo_ref[...], high)
        )
        back_f32[:, 2 * slot, :] = result[:, :half]
        back_f32[:, 2 * slot + 1, :] = result[:, half:]
    back_bf[...] = back_f32[...].astype(BF16)

    @for_peers
    def _(peer):
        pltpu.make_async_remote_copy(
            src_ref=back_bf.at[peer],
            dst_ref=home_bf.at[me],
            send_sem=back_send_sem,
            recv_sem=back_recv_sem,
            device_id={"seq": peer},
            device_id_type=MESH,
        ).start()

    home_bf[pl.ds(me, 1)] = back_bf[pl.ds(me, 1)]
    direct = skip_ref[...] * mixed.astype(F32)
    scale = gate_ref[...].astype(F32) * keep
    whole = home_bf.at[pl.ds(0, groups - 1)]
    pltpu.make_async_copy(whole, whole, back_recv_sem).wait()

    home = home_bf[...].astype(F32).reshape(2 * width, half).astype(BF16)
    slot_id = lax.broadcasted_iota(jnp.int32, (2 * width, width), 0)
    chan_id = lax.broadcasted_iota(jnp.int32, (2 * width, width), 1)
    for part in range(2):
        pick = (slot_id == 2 * chan_id + part).astype(F32).astype(BF16)
        conv = dot(home, pick, ((0,), (0,)))
        span = slice(part * half, (part + 1) * half)
        gated = (scale[span] * (conv + direct[span])).astype(BF16)
        gated_all[pl.ds(mine, 1), span, :] = gated.reshape(1, half, width)

    sends = []
    piece = rows // PIECES

    def gated_copy(source, part, peer):
        block = gated_all.at[source, pl.ds(part * piece, piece)]
        copy = pltpu.make_async_remote_copy(
            src_ref=block,
            dst_ref=block,
            send_sem=gated_send_sem.at[len(sends)],
            recv_sem=gated_recv_sem.at[source, part],
            device_id={"chan": peer},
            device_id_type=MESH,
        )
        copy.start()
        sends.append(copy)

    def arrived(source, part):
        block = gated_all.at[source, pl.ds(part * piece, piece)]
        pltpu.make_async_copy(block, block, gated_recv_sem.at[source, part]).wait()

    right, far, left = [lax.rem(mine + 2 * step, chans) for step in (1, 2, 3)]
    via, back = left, right
    gated_copy(mine, 1, via)
    gated_copy(mine, 0, far)
    gated_copy(mine, 0, via)
    gated_copy(mine, 0, back)
    gated_copy(mine, 1, back)
    for part in range(PIECES):
        gated_copy(mine, part, sibling)

    whole = weight_all.at[pl.ds(0, chans - 1)]
    pltpu.make_async_copy(whole, whole, weight_recv_sem).wait()

    def term(source):
        return dot(gated_all[source], weight_all[source], ((1,), (1,)))

    total = term(mine)
    for part in range(PIECES):
        arrived(sibling, part)
    total += term(sibling)
    arrived(back, 1)
    gated_copy(back, 1, via)
    gated_copy(back, 1, sibling)
    for source, part in ((back, 0), (via, 0), (far, 0), (via, 1), (far, 1)):
        arrived(source, part)
        gated_copy(source, part, sibling)
    for source in (far, left, right):
        total += term(source)
    for source in (far, left, right):
        other = source + 1 - 2 * core
        for part in range(PIECES):
            arrived(other, part)
        total += term(other)
    out_ref[...] = total.astype(BF16)

    for send in sends:
        send.wait_send()
    for block, sem, count in (
        (in_bf, send_sem, groups - 1),
        (home_bf, back_send_sem, groups - 1),
        (weight_all, weight_send_sem, chans - 1),
    ):
        whole = block.at[pl.ds(0, count)]
        pltpu.make_async_copy(whole, whole, sem).wait()


def on_device(signal_in, value_in, gate_in, filter_taps, skip_gain, turn_starts, out_weight):
    rows, width = signal_in.shape
    groups = lax.axis_size("seq")
    chans = lax.axis_size("chan")
    own = width // groups
    tables = [jnp.asarray(table) for table in make_tables(groups, rows)]
    held = (
        signal_in,
        value_in,
        gate_in,
        filter_taps,
        skip_gain.reshape(1, width),
        turn_starts.reshape(1, -1),
        *tables,
    )
    dma = pltpu.SemaphoreType.DMA
    return pl.pallas_call(
        functools.partial(kernel, groups, chans),
        out_shape=jax.ShapeDtypeStruct((rows, width), BF16),
        in_specs=[pl.BlockSpec(memory_space=pl.ANY)] * (7 + len(tables)),
        out_specs=pl.BlockSpec(memory_space=pltpu.VMEM),
        scratch_shapes=[
            pltpu.VMEM((groups, 2 * own, rows), BF16),
            pltpu.VMEM((groups, 2 * own, rows), BF16),
            pltpu.VMEM((groups, 2 * own, rows), F32),
            pltpu.VMEM((2 * own * groups, 2 * rows), BF16),
            pltpu.VMEM((2 * own * groups, 2 * rows), BF16),
            pltpu.VMEM((groups, 2 * own, rows // 2), F32),
            pltpu.VMEM((groups, 2 * own, rows // 2), BF16),
            pltpu.VMEM((groups, 2 * own, rows // 2), BF16),
            pltpu.VMEM((chans, rows, width), BF16),
            pltpu.VMEM((chans, width, width), BF16),
            *[pltpu.VMEM(array.shape, array.dtype) for array in held],
            dma((len(held) + 1,)),
            dma,
            dma,
            dma,
            dma,
            dma,
            dma,
            dma((7 * PIECES,)),
            dma((chans, PIECES)),
        ],
        compiler_params=pltpu.CompilerParams(collective_id=0, has_side_effects=True),
    )(*held[:6], out_weight, *held[6:])


def solution(mesh):
    in_specs = (
        P("seq", "chan"),
        P("seq", "chan"),
        P("seq", "chan"),
        P("seq", "chan"),
        P("chan"),
        P(),
        P(None, "chan"),
    )
    out_specs = P("seq", "chan")
    return jax.shard_map(
        on_device, mesh=mesh, in_specs=in_specs, out_specs=out_specs, check_vma=False
    )
```

```python
import functools
import math

import jax
import jax.numpy as jnp
import ml_dtypes
import numpy as np
from jax import lax
from jax.experimental import pallas as pl
from jax.experimental.pallas import tpu as pltpu
from jax.sharding import PartitionSpec as P

PIECES = 2
MESH = pl.DeviceIdType.MESH
F32 = jnp.float32
BF16 = jnp.bfloat16


def split_table(table):
    high = table.astype(ml_dtypes.bfloat16)
    low = (table - high.astype(np.float64)).astype(ml_dtypes.bfloat16)
    return high, low


def make_tables(groups, rows):
    length = 2 * groups * rows
    outer = np.arange(groups)
    inner = np.arange(rows)
    odd = 2 * outer + 1
    angle = 2.0 * math.pi * (odd[:, None] * outer[None, :] % (4 * groups)) / (4 * groups)
    first = np.concatenate([np.cos(angle), -np.sin(angle)], axis=0)
    twist = 2.0 * math.pi * (odd[:, None] * inner[None, :] % (2 * length)) / (2 * length)
    angle = 2.0 * math.pi * (inner[:, None] * inner[None, :] % rows) / rows
    cos, sin = np.cos(angle), np.sin(angle)
    middle = np.block([[cos, -sin], [sin, cos]])
    last = first.T * (2.0 / length)
    return (
        *split_table(first),
        *split_table(last),
        *split_table(middle),
        np.cos(twist).astype(np.float32),
        np.sin(twist).astype(np.float32),
    )


def halves(value):
    high = value.astype(BF16)
    return high, (value - high.astype(F32)).astype(BF16)


def dot(left, right, dims=((1,), (0,))):
    return lax.dot_general(left, right, (dims, ((), ())), preferred_element_type=F32)


def farthest(step, size):
    return (size // 2 + (1 - 2 * (step % 2)) * ((step + 1) // 2)) % size


def kernel(
    groups,
    chans,
    signal_hbm,
    value_hbm,
    gate_hbm,
    taps_hbm,
    skip_hbm,
    starts_hbm,
    weight_ref,
    first_hi_hbm,
    first_lo_hbm,
    last_hi_hbm,
    last_lo_hbm,
    mid_hi_hbm,
    mid_lo_hbm,
    twist_cos_hbm,
    twist_sin_hbm,
    out_ref,
    out_bf,
    in_bf,
    in_f32,
    spec_hi,
    spec_lo,
    back_f32,
    back_bf,
    home_bf,
    gated_all,
    weight_all,
    signal_ref,
    value_ref,
    gate_ref,
    taps_ref,
    skip_ref,
    starts_ref,
    first_hi_ref,
    first_lo_ref,
    last_hi_ref,
    last_lo_ref,
    mid_hi_ref,
    mid_lo_ref,
    twist_cos_ref,
    twist_sin_ref,
    load_sem,
    send_sem,
    recv_sem,
    back_send_sem,
    back_recv_sem,
    weight_send_sem,
    weight_recv_sem,
    gated_send_sem,
    gated_recv_sem,
):
    rows, width = signal_hbm.shape
    own = width // groups
    half = rows // 2
    side = math.isqrt(groups)
    me = lax.axis_index("seq")
    mine = lax.axis_index("chan")
    row, col = me // side, lax.rem(me, side)
    core = lax.rem(mine, 2)
    sibling = mine + 1 - 2 * core

    cols = [lax.rem(col + farthest(step, side), side) for step in range(side)]

    bases = [lax.rem(row + farthest(step, side), side) * side for step in range(side - 1)]

    def for_peers(act):
        for base in bases:
            for other in cols:
                act(base + other)

        for other in cols[:-1]:
            act(row * side + other)

    barrier = pltpu.get_barrier_semaphore()

    @for_peers
    def _(peer):
        pl.semaphore_signal(barrier, inc=1, device_id={"seq": peer}, device_id_type=MESH)

    @pl.loop(1, chans)
    def _(step):
        pl.semaphore_signal(
            barrier, inc=1, device_id={"chan": lax.rem(mine + step, chans)}, device_id_type=MESH
        )

    held = (
        (signal_hbm, signal_ref),
        (value_hbm, value_ref),
        (gate_hbm, gate_ref),
        (taps_hbm, taps_ref),
        (skip_hbm, skip_ref),
        (starts_hbm, starts_ref),
        (first_hi_hbm, first_hi_ref),
        (first_lo_hbm, first_lo_ref),
        (last_hi_hbm, last_hi_ref),
        (last_lo_hbm, last_lo_ref),
        (mid_hi_hbm, mid_hi_ref),
        (mid_lo_hbm, mid_lo_ref),
        (twist_cos_hbm, twist_cos_ref),
        (twist_sin_hbm, twist_sin_ref),
    )
    loads = [
        pltpu.make_async_copy(source, target, load_sem.at[place])
        for place, (source, target) in enumerate(held)
    ]
    loads.append(
        pltpu.make_async_copy(
            weight_ref.at[pl.ds(mine * width, width)], weight_all.at[mine], load_sem.at[len(held)]
        )
    )
    for load in loads:
        load.start()
    for place in (0, 1, 3):
        loads[place].wait()

    mixed = (signal_ref[...].astype(F32) * value_ref[...].astype(F32)).astype(BF16)
    row_id = lax.broadcasted_iota(jnp.int32, (2 * width, width), 0)
    col_id = lax.broadcasted_iota(jnp.int32, (2 * width, width), 1)
    target = 2 * own * (col_id // own) + lax.rem(col_id, own)
    pick_signal = (row_id == target).astype(F32).astype(BF16)
    pick_taps = (row_id == target + own).astype(F32).astype(BF16)
    turned = dot(pick_signal, mixed, ((1,), (1,))) + dot(pick_taps, taps_ref[...], ((1,), (1,)))
    out_bf[...] = turned.reshape(groups, 2 * own, rows).astype(BF16)

    pl.semaphore_wait(barrier, groups + chans - 2)

    @for_peers
    def _(peer):
        pltpu.make_async_remote_copy(
            src_ref=out_bf.at[peer],
            dst_ref=in_bf.at[me],
            send_sem=send_sem,
            recv_sem=recv_sem,
            device_id={"seq": peer},
            device_id_type=MESH,
        ).start()

    @pl.loop(1, chans)
    def _(step):
        peer = lax.rem(mine + step, chans)
        pltpu.make_async_remote_copy(
            src_ref=weight_ref.at[pl.ds(peer * width, width)],
            dst_ref=weight_all.at[mine],
            send_sem=weight_send_sem,
            recv_sem=weight_recv_sem,
            device_id={"chan": peer},
            device_id_type=MESH,
        ).start()

    in_bf[pl.ds(me, 1)] = out_bf[pl.ds(me, 1)]
    for place in (2, *range(4, len(loads))):
        loads[place].wait()
    positions = me * rows + lax.broadcasted_iota(jnp.int32, (rows, starts_ref.shape[1]), 0)
    counted = jnp.sum(
        jnp.where(starts_ref[...] <= positions, 1.0, 0.0).astype(F32), axis=1, keepdims=True
    )
    keep = counted - 2.0 * jnp.floor(0.5 * counted)
    twist_cos = twist_cos_ref[...]
    twist_sin = twist_sin_ref[...]

    whole = in_bf.at[pl.ds(0, groups - 1)]
    pltpu.make_async_copy(whole, whole, recv_sem).wait()

    in_f32[...] = in_bf[...].astype(F32)
    for slot in range(2 * own):
        data = in_f32[:, slot, :].astype(BF16)
        raw = dot(first_hi_ref[...], data) + dot(first_lo_ref[...], data)
        real, imag = raw[:groups], raw[groups:]
        here = pl.ds(slot * groups, groups)
        spec_hi[here, :rows], spec_lo[here, :rows] = halves(real * twist_cos + imag * twist_sin)
        spec_hi[here, rows:], spec_lo[here, rows:] = halves(imag * twist_cos - real * twist_sin)
    spectrum = (
        dot(spec_hi[...], mid_hi_ref[...])
        + dot(spec_lo[...], mid_hi_ref[...])
        + dot(spec_hi[...], mid_lo_ref[...])
    )
    middle = own * groups
    z_re, z_im = spectrum[:middle, :rows], spectrum[:middle, rows:]
    h_re, h_im = spectrum[middle:, :rows], spectrum[middle:, rows:]
    prod_hi, prod_lo = halves(
        jnp.concatenate([z_re * h_re - z_im * h_im, z_re * h_im + z_im * h_re], axis=1)
    )
    inverse = (
        dot(prod_hi, mid_hi_ref[...], ((1,), (1,)))
        + dot(prod_lo, mid_hi_ref[...], ((1,), (1,)))
        + dot(prod_hi, mid_lo_ref[...], ((1,), (1,)))
    )
    for slot in range(own):
        real = inverse[slot * groups : (slot + 1) * groups, :rows]
        imag = inverse[slot * groups : (slot + 1) * groups, rows:]
        high, low = halves(
            jnp.concatenate(
                [real * twist_cos - imag * twist_sin, imag * twist_cos + real * twist_sin], axis=0
            )
        )
        result = (
            dot(last_hi_ref[...], high) + dot(last_hi_ref[...], low) + dot(last_lo_ref[...], high)
        )
        back_f32[:, 2 * slot, :] = result[:, :half]
        back_f32[:, 2 * slot + 1, :] = result[:, half:]
    back_bf[...] = back_f32[...].astype(BF16)

    @for_peers
    def _(peer):
        pltpu.make_async_remote_copy(
            src_ref=back_bf.at[peer],
            dst_ref=home_bf.at[me],
            send_sem=back_send_sem,
            recv_sem=back_recv_sem,
            device_id={"seq": peer},
            device_id_type=MESH,
        ).start()

    home_bf[pl.ds(me, 1)] = back_bf[pl.ds(me, 1)]
    picks = [(row_id == 2 * col_id + part).astype(F32).astype(BF16) for part in range(2)]
    direct = skip_ref[...] * mixed.astype(F32)
    scale = gate_ref[...].astype(F32) * keep
    whole = home_bf.at[pl.ds(0, groups - 1)]
    pltpu.make_async_copy(whole, whole, back_recv_sem).wait()

    home = home_bf[...].astype(F32).reshape(2 * width, half).astype(BF16)
    for part in range(2):
        conv = dot(home, picks[part], ((0,), (0,)))
        span = slice(part * half, (part + 1) * half)
        gated = (scale[span] * (conv + direct[span])).astype(BF16)
        gated_all[pl.ds(mine, 1), span, :] = gated.reshape(1, half, width)

    sends = []
    piece = rows // PIECES

    def gated_copy(source, part, peer):
        block = gated_all.at[source, pl.ds(part * piece, piece)]
        copy = pltpu.make_async_remote_copy(
            src_ref=block,
            dst_ref=block,
            send_sem=gated_send_sem.at[len(sends)],
            recv_sem=gated_recv_sem.at[source, part],
            device_id={"chan": peer},
            device_id_type=MESH,
        )
        copy.start()
        sends.append(copy)

    def arrived(source, part):
        block = gated_all.at[source, pl.ds(part * piece, piece)]
        pltpu.make_async_copy(block, block, gated_recv_sem.at[source, part]).wait()

    right, far, left = [lax.rem(mine + 2 * step, chans) for step in (1, 2, 3)]
    via, back = left, right
    gated_copy(mine, 1, via)
    gated_copy(mine, 0, far)
    gated_copy(mine, 0, via)
    gated_copy(mine, 0, back)
    gated_copy(mine, 1, back)
    for part in range(PIECES):
        gated_copy(mine, part, sibling)

    whole = weight_all.at[pl.ds(0, chans - 1)]
    pltpu.make_async_copy(whole, whole, weight_recv_sem).wait()

    def term(source):
        return dot(gated_all[source], weight_all[source], ((1,), (1,)))

    total = term(mine)
    for part in range(PIECES):
        arrived(sibling, part)
    total += term(sibling)
    arrived(back, 1)
    gated_copy(back, 1, via)
    gated_copy(back, 1, sibling)
    for source, part in ((back, 0), (via, 0), (far, 0), (via, 1), (far, 1)):
        arrived(source, part)
        gated_copy(source, part, sibling)
    for source in (far, left, right):
        total += term(source)
    for source in (far, left, right):
        other = source + 1 - 2 * core
        for part in range(PIECES):
            arrived(other, part)
        total += term(other)
    out_ref[...] = total.astype(BF16)

    for send in sends:
        send.wait_send()
    for block, sem, count in (
        (in_bf, send_sem, groups - 1),
        (home_bf, back_send_sem, groups - 1),
        (weight_all, weight_send_sem, chans - 1),
    ):
        whole = block.at[pl.ds(0, count)]
        pltpu.make_async_copy(whole, whole, sem).wait()


def on_device(signal_in, value_in, gate_in, filter_taps, skip_gain, turn_starts, out_weight):
    rows, width = signal_in.shape
    groups = lax.axis_size("seq")
    chans = lax.axis_size("chan")
    own = width // groups
    tables = [jnp.asarray(table) for table in make_tables(groups, rows)]
    held = (
        signal_in,
        value_in,
        gate_in,
        filter_taps,
        skip_gain.reshape(1, width),
        turn_starts.reshape(1, -1),
        *tables,
    )
    dma = pltpu.SemaphoreType.DMA
    return pl.pallas_call(
        functools.partial(kernel, groups, chans),
        out_shape=jax.ShapeDtypeStruct((rows, width), BF16),
        in_specs=[pl.BlockSpec(memory_space=pl.ANY)] * (7 + len(tables)),
        out_specs=pl.BlockSpec(memory_space=pltpu.VMEM),
        scratch_shapes=[
            pltpu.VMEM((groups, 2 * own, rows), BF16),
            pltpu.VMEM((groups, 2 * own, rows), BF16),
            pltpu.VMEM((groups, 2 * own, rows), F32),
            pltpu.VMEM((2 * own * groups, 2 * rows), BF16),
            pltpu.VMEM((2 * own * groups, 2 * rows), BF16),
            pltpu.VMEM((groups, 2 * own, rows // 2), F32),
            pltpu.VMEM((groups, 2 * own, rows // 2), BF16),
            pltpu.VMEM((groups, 2 * own, rows // 2), BF16),
            pltpu.VMEM((chans, rows, width), BF16),
            pltpu.VMEM((chans, width, width), BF16),
            *[pltpu.VMEM(array.shape, array.dtype) for array in held],
            dma((len(held) + 1,)),
            dma,
            dma,
            dma,
            dma,
            dma,
            dma,
            dma((7 * PIECES,)),
            dma((chans, PIECES)),
        ],
        compiler_params=pltpu.CompilerParams(collective_id=0, has_side_effects=True),
    )(*held[:6], out_weight, *held[6:])


def solution(mesh):
    in_specs = (
        P("seq", "chan"),
        P("seq", "chan"),
        P("seq", "chan"),
        P("seq", "chan"),
        P("chan"),
        P(),
        P(None, "chan"),
    )
    out_specs = P("seq", "chan")
    return jax.shard_map(
        on_device, mesh=mesh, in_specs=in_specs, out_specs=out_specs, check_vma=False
    )
```
